32 devices in a mesh: fsdp: 8 (over y, x, core), tp: 4 (over z).
Axes of the slice: x: 2, y: 2, z: 4, core: 2. Of those that a mesh axis runs over, the one named last changes fastest.
Arguments:
- features: bfloat16 [1024, 8192], P('fsdp'), may hold values from -17 to 17
- key_partials: bfloat16 [1024, 4, 128], P('fsdp', 'tp'), may hold values from -0.30935922 to 0.30935922
- momentum: float32 [4096, 4, 128], P('fsdp', 'tp'), may hold values from -6 to 6
Outputs:
- update: float32 [4096, 4, 128], P('fsdp', 'tp')
- new_momentum: float32 [4096, 4, 128], P('fsdp', 'tp')
The draws below stay inside these ranges and needn't reach their ends.
All inputs are finite; a program needn't handle non-finite values.
Results may differ from the reference program's by a relative error of at most 0.0003.
Values may be sent and summed in bfloat16 or wider, within the bound.
No kernel may reach another device: no remote copies, remote signals or barrier semaphores. Data moves between devices by JAX's collectives and lax.ppermute only.
A program may use at most 64 MiB of HBM per device.

```python
import math
import jax
import jax.numpy as jnp
from jax import lax

D_W = 8192
HD = 128
ITERS = 5
KVH = 2
TOKENS = 1024
N_FSDP = 8
N_TP = 4


def draw_features(key, part):
    first = jax.random.fold_in(jax.random.fold_in(key, 11), 0)
    columns = jnp.arange(D_W, dtype=jnp.float32) / D_W
    base = jnp.clip(jax.random.normal(first, (TOKENS, D_W), jnp.float32), -5.0, 5.0)
    scales = jnp.sqrt(1.0 + 2.0 * columns)
    return (base * scales[None, :]).astype(jnp.bfloat16)


def draw_key_partials(key, part):
    first = jax.random.fold_in(jax.random.fold_in(key, 23), 0)
    factor = (2.0 * TOKENS) ** (-0.5)
    values = jnp.clip(jax.random.normal(first, (TOKENS, N_TP, HD), jnp.float32), -4.0, 4.0) * factor
    return values.astype(jnp.bfloat16)


def levels(rng, dims, shards, least, largest):
    gain, own = 1.0, jax.random.fold_in(rng, 6)
    for axis_at, blocks in shards:
        heights = jnp.exp(jax.random.uniform(jax.random.fold_in(own, axis_at), (blocks,), jnp.float32, least / len(shards), largest / len(shards)))
        gain = gain * jnp.repeat(heights, dims[axis_at] // blocks).reshape([-1 if axis == axis_at else 1 for axis in range(len(dims))])
    return gain


def noise(rng, extent, scale, most, shards=(), held_as=jnp.bfloat16):
    entries = scale * jax.random.normal(rng, extent, jnp.float32)
    if shards:
        entries = entries * levels(rng, extent, shards, -0.22, 0.18)
    return jnp.clip(entries, -most, most).astype(held_as)


def setup_inputs(seed: int = 0) -> dict:
    key_of = jax.random.split(jax.random.key(seed), 4)
    features = draw_features(jax.random.fold_in(key_of[3], 71), 0)
    key_partials = draw_key_partials(jax.random.fold_in(key_of[3], 71), 0)
    momentum = noise(key_of[2], (D_W // 2, N_TP, HD), 1.0, 6.0, ((0, 8), (1, 4)), jnp.float32)
    return {"features": features, "key_partials": key_partials, "momentum": momentum}


retain = 0.95
first_coef = 3.4445
second_coef = -4.775
third_coef = 2.0315
epsilon = 1e-07
shrink = 0.2

def dense_layout(stored):
    halves = D_W // (2 * N_FSDP)
    return stored.reshape(N_FSDP, halves, KVH, 2, HD).transpose(2, 0, 3, 1, 4).reshape(KVH, D_W, HD)

def stored_layout(dense):
    halves = D_W // (2 * N_FSDP)
    return dense.reshape(KVH, N_FSDP, 2, halves, HD).transpose(1, 3, 0, 2, 4).reshape(N_FSDP * halves, KVH * 2, HD)

def reference(features, key_partials, momentum):
    precise = lax.Precision.HIGHEST
    widened = features.astype(jnp.float32)
    summed = key_partials.astype(jnp.float32).reshape(TOKENS, KVH, 2, HD).sum(axis=2).reshape(TOKENS, KVH * HD)
    grads = lax.dot_general(widened, summed, (((0,), (0,)), ((), ())), precision=precise)
    grads = grads.reshape(D_W, KVH, HD).transpose(1, 0, 2)
    moment = dense_layout(momentum)
    fresh = retain * moment + grads
    blend = grads + retain * fresh
    length = jnp.sqrt(lax.optimization_barrier(jnp.sum(blend * blend, axis=(1, 2), keepdims=True)))
    state = blend / (length + epsilon)
    for step in range(ITERS):
        gram = jnp.einsum('hrd,hre->hde', state, state, precision=precise)
        square = jnp.einsum('hde,hef->hdf', gram, gram, precision=precise)
        poly = second_coef * gram + third_coef * square
        state = first_coef * state + jnp.einsum('hrd,hde->hre', state, poly, precision=precise)
    update = shrink * math.sqrt(D_W) * state
    return (stored_layout(update), stored_layout(fresh))
```

```python
import math

import jax
import jax.numpy as jnp
from jax import lax
from jax.experimental import pallas as pl
from jax.experimental.pallas import tpu as pltpu
from jax.sharding import PartitionSpec as P

ITERS = 5


retain = 0.95
first_coef = 3.4445
second_coef = -4.775
third_coef = 2.0315
epsilon = 1e-07
shrink = 0.2
precise = lax.Precision.HIGHEST
contract = (((0,), (0,)), ((), ()))


def swapped(block, fsdp_bits, tp_bits):
    n_tp = lax.axis_size("tp")
    count = lax.axis_size("fsdp") * n_tp
    mask = fsdp_bits * n_tp + tp_bits
    return lax.ppermute(block, ("fsdp", "tp"), [(i, i ^ mask) for i in range(count)])


def finish(grads, moment_ref, fresh_ref, blend_ref, gram_ref):
    fresh = retain * moment_ref[...] + grads
    blend = grads + retain * fresh
    fresh_ref[...] = fresh
    blend_ref[...] = blend
    gram_ref[...] = lax.dot_general(blend, blend, contract, precision=precise)


def pack_kernel(width, starts_ref, features_ref, *refs):
    outs, sems = refs[:-1], refs[-1]
    copies = []
    for i, out in enumerate(outs):
        for j in range(2):
            start = pl.multiple_of(starts_ref[2 * i + j], width)
            copies.append(
                pltpu.make_async_copy(
                    features_ref.at[:, pl.ds(start, width)],
                    out.at[:, pl.ds(j * width, width)],
                    sems.at[2 * i + j],
                )
            )
    for copy in copies:
        copy.start()
    for copy in copies:
        copy.wait()


def partial_kernel(n_pieces, *refs):
    features, keys = refs[:n_pieces], refs[n_pieces : 2 * n_pieces]
    partner_ref, mine_ref, other_ref = refs[2 * n_pieces :]
    tokens, head_size = keys[0].shape
    grads = None
    for i, (piece, key) in enumerate(zip(features, keys)):
        both = jnp.concatenate([key[...], partner_ref[i * tokens : (i + 1) * tokens, :]], axis=1)
        term = lax.dot_general(both, piece[...], contract, preferred_element_type=jnp.float32)
        grads = term if grads is None else grads + term
    grads = grads[:head_size] + grads[head_size:]
    rows = mine_ref.shape[1]
    mine_ref[...] = grads[:, :rows]
    other_ref[...] = grads[:, rows:]


def joined_kernel(mine_ref, other_ref, moment_ref, fresh_ref, blend_ref, gram_ref):
    finish((mine_ref[...] + other_ref[...]).T, moment_ref, fresh_ref, blend_ref, gram_ref)


def plain_kernel(mine_ref, other_ref, moment_ref, fresh_ref, blend_ref, gram_ref):
    finish(mine_ref[...] + other_ref[...], moment_ref, fresh_ref, blend_ref, gram_ref)


def newton_kernel(scale, n_grams, *refs):
    grams, blend_ref, update_ref = refs[:n_grams], refs[n_grams], refs[n_grams + 1]
    gram = grams[0][...]
    for ref in grams[1:]:
        gram = gram + ref[...]
    size = gram.shape[0]
    rows = lax.broadcasted_iota(jnp.int32, (size, size), 0)
    columns = lax.broadcasted_iota(jnp.int32, (size, size), 1)
    diagonal = rows == columns
    total = jnp.sum(jnp.where(diagonal, gram, 0.0), axis=(0, 1), keepdims=True)
    inverse = 1.0 / (jnp.sqrt(total) + epsilon)
    gram = gram * (inverse * inverse)
    start = jnp.where(diagonal, first_coef, 0.0)
    product = None
    for step in range(ITERS):
        square = jnp.dot(gram, gram, precision=precise)
        poly = start + second_coef * gram + third_coef * square
        product = poly if product is None else jnp.dot(product, poly, precision=precise)
        if step + 1 < ITERS:
            gram = jnp.dot(jnp.dot(gram, poly, precision=precise), poly, precision=precise)
    update_ref[...] = jnp.dot(blend_ref[...] * inverse, product, precision=precise) * scale


def whole(count):
    return [pl.BlockSpec(memory_space=pltpu.VMEM) for _ in range(count)]


def on_device(features, key_partials, momentum):
    n_fsdp = lax.axis_size("fsdp")
    n_tp = lax.axis_size("tp")
    parity = lax.axis_index("tp") % 2
    index = lax.axis_index("fsdp")
    own_part = key_partials[:, 0, :]
    moment = momentum[:, 0, :]
    tokens, head_size = own_part.shape
    rows_half = moment.shape[0]
    bits = [1 << b for b in reversed(range(n_fsdp.bit_length() - 1))]
    direct = n_fsdp == 1 << len(bits) and n_fsdp <= 16 and rows_half % 128 == 0 and n_tp & (n_tp - 1) == 0
    block = jax.ShapeDtypeStruct((rows_half, head_size), jnp.float32)
    small = jax.ShapeDtypeStruct((head_size, head_size), jnp.float32)
    if direct:
        n_chip = n_fsdp // 2
        chip, core = index // 2, index % 2

        def starts_for(distance):
            first = ((chip ^ distance) * 2 + core) * 2 + parity
            second = ((chip ^ distance) * 2 + 1 - core) * 2 + parity
            return [first * rows_half, second * rows_half]

        distances = [d for d in range(n_chip)]
        starts = jnp.stack([s for d in distances for s in starts_for(d)]).astype(jnp.int32)
        packed = jax.ShapeDtypeStruct((tokens, 2 * rows_half), features.dtype)
        pieces = pl.pallas_call(
            lambda *refs: pack_kernel(rows_half, *refs),
            out_shape=(packed,) * n_chip,
            in_specs=[pl.BlockSpec(memory_space=pltpu.SMEM), pl.BlockSpec(memory_space=pl.ANY)],
            out_specs=tuple(whole(n_chip)),
            scratch_shapes=[pltpu.SemaphoreType.DMA((2 * n_chip,))],
            name="pack",
        )(starts, features)
        keys = [own_part if d == 0 else swapped(own_part, 2 * d, 0) for d in distances]
        partner_keys = swapped(jnp.concatenate(keys, axis=0), 0, 1)
        pieces = [pieces[d] if d == 0 else swapped(pieces[d], 2 * d, 0) for d in distances]
        half = jax.ShapeDtypeStruct((head_size, rows_half), jnp.float32)
        mine, other = pl.pallas_call(
            lambda *refs: partial_kernel(n_chip, *refs),
            out_shape=(half, half),
            in_specs=whole(2 * n_chip + 1),
            out_specs=tuple(whole(2)),
            name="partial",
        )(*pieces, *keys, partner_keys)
        fresh, blend, gram = pl.pallas_call(
            joined_kernel,
            out_shape=(block, block, small),
            in_specs=whole(3),
            out_specs=tuple(whole(3)),
            name="gradient",
        )(mine, swapped(other, 1, 0), moment)
        for bit in reversed(bits):
            gram = gram + swapped(gram, bit, 0)
        grams = [gram, swapped(gram, 0, 1)]
    else:
        shard = lax.psum_scatter(
            lax.dot_general(features, own_part, contract, preferred_element_type=jnp.float32),
            "fsdp",
            scatter_dimension=0,
            tiled=True,
        )
        halves = shard.reshape(2, rows_half, head_size)
        mine = jnp.where(parity == 0, halves[0], halves[1])
        other = jnp.where(parity == 0, halves[1], halves[0])
        fresh, blend, gram = pl.pallas_call(
            plain_kernel,
            out_shape=(block, block, small),
            in_specs=whole(3),
            out_specs=tuple(whole(3)),
            name="gradient",
        )(mine, swapped(other, 0, 1), moment)
        gram = lax.psum(gram, "fsdp")
        grams = [gram, swapped(gram, 0, 1)]
    scale = shrink * math.sqrt(2 * n_fsdp * rows_half)
    update = pl.pallas_call(
        lambda *refs: newton_kernel(scale, len(grams), *refs),
        out_shape=block,
        in_specs=whole(len(grams) + 1),
        out_specs=whole(1)[0],
        name="newton",
    )(*grams, blend)
    return (update[:, None, :], fresh[:, None, :])


def solution(mesh):
    placed = (P("fsdp", None), P("fsdp", "tp", None), P("fsdp", "tp", None))
    return jax.shard_map(
        on_device,
        mesh=mesh,
        in_specs=placed,
        out_specs=(P("fsdp", "tp", None), P("fsdp", "tp", None)),
        check_vma=False,
    )
```

```python
import math

import jax
import jax.numpy as jnp
from jax import lax
from jax.experimental import pallas as pl
from jax.experimental.pallas import tpu as pltpu
from jax.sharding import PartitionSpec as P


ITERS = 5


retain = 0.95
first_coef = 3.4445
second_coef = -4.775
third_coef = 2.0315
epsilon = 1e-07
shrink = 0.2
contract = (((0,), (0,)), ((), ()))


def swapped(block, fsdp_bits, tp_bits):
    n_tp = lax.axis_size("tp")
    count = lax.axis_size("fsdp") * n_tp
    mask = fsdp_bits * n_tp + tp_bits
    return lax.ppermute(block, ("fsdp", "tp"), [(i, i ^ mask) for i in range(count)])


def halves(value):
    high = value.astype(jnp.bfloat16)
    return high, (value - high.astype(jnp.float32)).astype(jnp.bfloat16)


def thirds(value):
    high = value.astype(jnp.bfloat16)
    rest = value - high.astype(jnp.float32)
    middle = rest.astype(jnp.bfloat16)
    return high, middle, (rest - middle.astype(jnp.float32)).astype(jnp.bfloat16)


def product_of(left, right):
    l1, l2, l3 = left
    r1, r2, r3 = right
    columns = r1.shape[1]
    square = jnp.concatenate([jnp.concatenate([r1, r2], 1), jnp.concatenate([r2, r1], 1)], 0)
    main = jnp.dot(jnp.concatenate([l1, l2], 1), square, preferred_element_type=jnp.float32)
    rest = jnp.dot(jnp.concatenate([l1, l3], 1), jnp.concatenate([r3, r1], 0), preferred_element_type=jnp.float32)
    return (rest + main[:, columns:]) + main[:, :columns]


def gram_of(value):
    width = value.shape[1]
    both = jnp.concatenate(halves(value), axis=1)
    parts = lax.dot_general(both, both, contract, preferred_element_type=jnp.float32)
    cross = parts[:width, width:] + parts[width:, :width]
    return (parts[width:, width:] + cross) + parts[:width, :width]


def packed_gram(gram):
    half = gram.shape[0] // 2
    upper, corner = gram[:half], gram[half:, half:]
    shape = (half, half)
    rows, columns = (lax.broadcasted_iota(jnp.int32, shape, axis) for axis in range(2))
    left = jnp.where(rows >= columns, upper[:, :half], corner)
    diagonal = jnp.sum(jnp.where(rows == columns, corner, 0.0), axis=0, keepdims=True)
    diagonal = jnp.broadcast_to(jnp.concatenate([diagonal, diagonal], axis=1), (8, 2 * half))
    return jnp.concatenate([jnp.concatenate([left, upper[:, half:]], axis=1), diagonal], axis=0)


def unpacked_gram(packed):
    half = packed.shape[1] // 2
    left, right, diagonal = packed[:half, :half], packed[:half, half:], packed[half : half + 1, :half]
    rows, columns = (lax.broadcasted_iota(jnp.int32, (half, half), axis) for axis in range(2))
    weight = jnp.where(rows == columns, 0.5, 1.0)
    first = jnp.where(rows >= columns, left * weight, 0.0)
    second = jnp.where(rows < columns, left, jnp.where(rows == columns, 0.5 * diagonal, 0.0))
    top = jnp.concatenate([first, right], axis=1)
    bottom = jnp.concatenate([jnp.zeros((half, half), jnp.float32), second], axis=1)
    triangle = jnp.concatenate([top, bottom], axis=0)
    return triangle + triangle.T


def advanced(grads, moment):
    fresh = retain * moment + grads
    return fresh, grads + retain * fresh


def pack_kernel(width, features_ref, *refs):
    outs, sems = refs[:-1], refs[-1]
    index = lax.axis_index("fsdp")
    parity = lax.axis_index("tp") % 2
    chip, core = index // 2, index % 2
    copies = []
    for i, out in enumerate(outs):
        for j in range(2):
            block = (chip ^ i) * 2 + (core ^ j)
            start = pl.multiple_of((block * 2 + parity) * width, width)
            copies.append(
                pltpu.make_async_copy(
                    features_ref.at[:, pl.ds(start, width)],
                    out.at[:, pl.ds(j * width, width)],
                    sems.at[2 * i + j],
                )
            )
    for copy in copies:
        copy.start()
    for copy in copies:
        copy.wait()


def partial_kernel(n_pieces, *refs):
    features, keys = refs[:n_pieces], refs[n_pieces : 2 * n_pieces]
    partner_ref, grads_ref = refs[2 * n_pieces :]
    head_size = grads_ref.shape[1]
    own = jnp.concatenate([key[...] for key in keys], axis=0)
    keys = jnp.concatenate([own, partner_ref[...]], axis=1)
    features = jnp.concatenate([piece[...] for piece in features], axis=0)
    both = lax.dot_general(features, keys, contract, preferred_element_type=jnp.float32)
    grads_ref[...] = both[:, :head_size] + both[:, head_size:]


def joined_kernel(own_ref, other_ref, moment_ref, twin_ref, fresh_ref, blend_ref, gram_ref):
    rows = moment_ref.shape[0]
    fresh, blend = advanced(own_ref[:rows] + other_ref[rows:], moment_ref[...])
    twin = advanced(own_ref[rows:] + other_ref[:rows], twin_ref[...])[1]
    fresh_ref[...] = fresh
    blend_ref[...] = blend
    gram_ref[...] = packed_gram(gram_of(jnp.concatenate([blend, twin], axis=0)))


def plain_kernel(mine_ref, other_ref, moment_ref, fresh_ref, blend_ref, gram_ref):
    fresh, blend = advanced(mine_ref[...] + other_ref[...], moment_ref[...])
    fresh_ref[...] = fresh
    blend_ref[...] = blend
    gram_ref[...] = packed_gram(gram_of(blend))


def applied(value, factor):
    columns = factor.shape[1]
    left = jnp.concatenate(halves(value), axis=1)
    right = jnp.concatenate(halves(factor), axis=1)
    both = jnp.dot(left, jnp.concatenate([right, right], axis=0), preferred_element_type=jnp.float32)
    return both[:, columns:] + both[:, :columns]


def stacked(first, second):
    return tuple(jnp.concatenate(pair, axis=0) for pair in zip(first, second))


def newton_kernel(scale, n_grams, *refs):
    grams, blend_ref, update_ref, staged_ref, sems = refs[:n_grams], *refs[n_grams:]
    total = grams[0][...]
    for ref in grams[1:]:
        total = total + ref[...]
    gram = unpacked_gram(total)
    size = gram.shape[0]
    rows = lax.broadcasted_iota(jnp.int32, (size, size), 0)
    columns = lax.broadcasted_iota(jnp.int32, (size, size), 1)
    diagonal = rows == columns
    trace = jnp.sum(jnp.where(diagonal, gram, 0.0), axis=(0, 1), keepdims=True)
    inverse = 1.0 / (jnp.sqrt(trace) + epsilon)
    gram = gram * (inverse * inverse)
    start = jnp.where(diagonal, first_coef, 0.0)
    product = None
    for _ in range(ITERS - 1):
        split = thirds(gram)
        square = product_of(split, split)
        poly = start + second_coef * gram + third_coef * square
        factor = thirds(poly)
        if product is None:
            product, turned = poly, product_of(split, factor)
        else:
            both = product_of(stacked(split, thirds(product)), factor)
            turned, product = both[:size], both[size:]
        gram = product_of(thirds(turned), factor)
    split = thirds(gram)
    poly = start + second_coef * gram + third_coef * product_of(split, split)
    partway = applied(blend_ref[...], product * (inverse * scale))
    chunk = partway.shape[0] // 4
    copies = []
    for i in range(4):
        part = pl.ds(i * chunk, chunk)
        staged_ref[part, :] = applied(partway[i * chunk : (i + 1) * chunk], poly)
        copies.append(pltpu.make_async_copy(staged_ref.at[part], update_ref.at[part], sems.at[i]))
        copies[-1].start()
    for copy in copies:
        copy.wait()


def whole(count):
    return [pl.BlockSpec(memory_space=pltpu.VMEM) for _ in range(count)]


def on_chip(*arrays):
    return [pltpu.with_memory_space_constraint(array, pltpu.VMEM) for array in arrays]


def ordered(features, key_partials, momentum):
    n_fsdp = lax.axis_size("fsdp")
    n_tp = lax.axis_size("tp")
    parity = lax.axis_index("tp") % 2
    own_part = key_partials[:, 0, :]
    moment = momentum[:, 0, :]
    tokens, head_size = own_part.shape
    rows_half = moment.shape[0]
    bits = [1 << b for b in reversed(range(n_fsdp.bit_length() - 1))]
    direct = n_fsdp == 1 << len(bits) and n_fsdp <= 16 and rows_half % 128 == 0 and n_tp & (n_tp - 1) == 0
    block = pltpu.VMEM((rows_half, head_size), jnp.float32)
    small = pltpu.VMEM((head_size // 2 + 8, head_size), jnp.float32)
    if direct:
        n_chip = n_fsdp // 2
        packed = pltpu.VMEM((tokens, 2 * rows_half), features.dtype)
        pieces = pl.pallas_call(
            lambda *refs: pack_kernel(rows_half, *refs),
            out_shape=(packed,) * n_chip,
            in_specs=[pl.BlockSpec(memory_space=pl.ANY)],
            out_specs=tuple(whole(n_chip)),
            scratch_shapes=[pltpu.SemaphoreType.DMA((2 * n_chip,))],
            name="pack",
        )(features)
        pieces, own_part = lax.optimization_barrier((pieces, own_part))
        pieces = list(pieces)
        for d in range(1, n_chip):
            pieces[d] = swapped(pieces[d], 2 * d, 0)
        keys = [own_part]
        for d in range(1, n_chip):
            keys.append(swapped(own_part, 2 * d, 0))
        partner_keys = swapped(jnp.concatenate(keys, axis=0), 0, 1)
        twin = swapped(moment, 1, 0)
        partner_keys, twin = lax.optimization_barrier((partner_keys, twin))
        grads = pl.pallas_call(
            lambda *refs: partial_kernel(n_chip, *refs),
            out_shape=pltpu.VMEM((2 * rows_half, head_size), jnp.float32),
            in_specs=whole(2 * n_chip + 1),
            out_specs=whole(1)[0],
            name="partial",
        )(*on_chip(*pieces, *keys, partner_keys))
        fresh, blend, gram = pl.pallas_call(
            joined_kernel,
            out_shape=(block, block, small),
            in_specs=whole(4),
            out_specs=tuple(whole(3)),
            name="gradient",
        )(*on_chip(grads, swapped(grads, 1, 0), moment, twin))
        for bit in bits[:-1]:
            gram = gram + swapped(gram, bit, 0)
        grams = [gram, swapped(gram, 0, 1)]
    else:
        shard = lax.psum_scatter(
            lax.dot_general(features, own_part, contract, preferred_element_type=jnp.float32),
            "fsdp",
            scatter_dimension=0,
            tiled=True,
        )
        pair = shard.reshape(2, rows_half, head_size)
        mine = jnp.where(parity == 0, pair[0], pair[1])
        other = jnp.where(parity == 0, pair[1], pair[0])
        fresh, blend, gram = pl.pallas_call(
            plain_kernel,
            out_shape=(block, block, small),
            in_specs=whole(3),
            out_specs=tuple(whole(3)),
            name="gradient",
        )(*on_chip(mine, swapped(other, 0, 1), moment))
        gram = lax.psum(gram, "fsdp")
        grams = [gram, swapped(gram, 0, 1)]
    scale = shrink * math.sqrt(2 * n_fsdp * rows_half)
    update = pl.pallas_call(
        lambda *refs: newton_kernel(scale, len(grams), *refs),
        out_shape=jax.ShapeDtypeStruct((rows_half, head_size), jnp.float32),
        in_specs=whole(len(grams) + 1),
        out_specs=pl.BlockSpec(memory_space=pl.ANY),
        scratch_shapes=[pltpu.VMEM((rows_half, head_size), jnp.float32), pltpu.SemaphoreType.DMA((4,))],
        name="newton",
    )(*on_chip(*grams, blend))
    return (update[:, None, :], fresh[:, None, :])


def solution(mesh):
    placed = (P("fsdp", None), P("fsdp", "tp", None), P("fsdp", "tp", None))
    return jax.shard_map(
        ordered,
        mesh=mesh,
        in_specs=placed,
        out_specs=(P("fsdp", "tp", None), P("fsdp", "tp", None)),
        check_vma=False,
    )
```

```python
import math

import jax
import jax.numpy as jnp
from jax import lax
from jax.experimental import pallas as pl
from jax.experimental.pallas import tpu as pltpu
from jax.sharding import PartitionSpec as P


ITERS = 5


retain = 0.95
first_coef = 3.4445
second_coef = -4.775
third_coef = 2.0315
epsilon = 1e-07
shrink = 0.2
contract = (((0,), (0,)), ((), ()))


def swapped(block, fsdp_bits, tp_bits):
    n_tp = lax.axis_size("tp")
    count = lax.axis_size("fsdp") * n_tp
    mask = fsdp_bits * n_tp + tp_bits
    return lax.ppermute(block, ("fsdp", "tp"), [(i, i ^ mask) for i in range(count)])


def halves(value):
    high = value.astype(jnp.bfloat16)
    return high, (value - high.astype(jnp.float32)).astype(jnp.bfloat16)


def thirds(value):
    high = value.astype(jnp.bfloat16)
    rest = value - high.astype(jnp.float32)
    middle = rest.astype(jnp.bfloat16)
    return high, middle, (rest - middle.astype(jnp.float32)).astype(jnp.bfloat16)


def product_of(left, right):
    l1, l2, l3 = left
    r1, r2, r3 = right
    columns = r1.shape[1]
    square = jnp.concatenate([jnp.concatenate([r1, r2], 1), jnp.concatenate([r2, r1], 1)], 0)
    main = jnp.dot(jnp.concatenate([l1, l2], 1), square, preferred_element_type=jnp.float32)
    rest = jnp.dot(jnp.concatenate([l1, l3], 1), jnp.concatenate([r3, r1], 0), preferred_element_type=jnp.float32)
    return (rest + main[:, columns:]) + main[:, :columns]


def gram_of(value):
    width = value.shape[1]
    both = jnp.concatenate(halves(value), axis=1)
    parts = lax.dot_general(both, both, contract, preferred_element_type=jnp.float32)
    cross = parts[:width, width:] + parts[width:, :width]
    return (parts[width:, width:] + cross) + parts[:width, :width]


def packed_gram(gram):
    half = gram.shape[0] // 2
    upper, corner = gram[:half], gram[half:, half:]
    shape = (half, half)
    rows, columns = (lax.broadcasted_iota(jnp.int32, shape, axis) for axis in range(2))
    left = jnp.where(rows >= columns, upper[:, :half], corner)
    diagonal = jnp.sum(jnp.where(rows == columns, corner, 0.0), axis=0, keepdims=True)
    diagonal = jnp.broadcast_to(jnp.concatenate([diagonal, diagonal], axis=1), (8, 2 * half))
    return jnp.concatenate([jnp.concatenate([left, upper[:, half:]], axis=1), diagonal], axis=0)


def unpacked_gram(packed):
    half = packed.shape[1] // 2
    left, right, diagonal = packed[:half, :half], packed[:half, half:], packed[half : half + 1, :half]
    rows, columns = (lax.broadcasted_iota(jnp.int32, (half, half), axis) for axis in range(2))
    weight = jnp.where(rows == columns, 0.5, 1.0)
    first = jnp.where(rows >= columns, left * weight, 0.0)
    second = jnp.where(rows < columns, left, jnp.where(rows == columns, 0.5 * diagonal, 0.0))
    top = jnp.concatenate([first, right], axis=1)
    bottom = jnp.concatenate([jnp.zeros((half, half), jnp.float32), second], axis=1)
    triangle = jnp.concatenate([top, bottom], axis=0)
    return triangle + triangle.T


def advanced(grads, moment):
    fresh = retain * moment + grads
    return fresh, grads + retain * fresh


def pack_kernel(width, features_ref, *refs):
    outs, sems = refs[:-1], refs[-1]
    index = lax.axis_index("fsdp")
    parity = lax.axis_index("tp") % 2
    chip, core = index // 2, index % 2
    copies = []
    for i, out in enumerate(outs):
        for j in range(2):
            block = (chip ^ i) * 2 + (core ^ j)
            start = pl.multiple_of((block * 2 + parity) * width, width)
            copies.append(
                pltpu.make_async_copy(
                    features_ref.at[:, pl.ds(start, width)],
                    out.at[:, pl.ds(j * width, width)],
                    sems.at[2 * i + j],
                )
            )
    for copy in copies:
        copy.start()
    for copy in copies:
        copy.wait()


def partial_kernel(n_pieces, *refs):
    features, keys, partner_ref, grads_ref = refs[:n_pieces], refs[n_pieces:-2], refs[-2], refs[-1]
    head_size = grads_ref.shape[1]
    own = jnp.concatenate([key[...] for key in keys], axis=0)
    keys = jnp.concatenate([own, partner_ref[...]], axis=1)
    features = jnp.concatenate([piece[...] for piece in features], axis=0)
    both = lax.dot_general(features, keys, contract, preferred_element_type=jnp.float32)
    grads_ref[...] = both[:, :head_size] + both[:, head_size:]


def joined_kernel(own_ref, other_ref, moment_ref, twin_ref, fresh_ref, blend_ref, gram_ref):
    rows = moment_ref.shape[0]
    fresh, blend = advanced(own_ref[:rows] + other_ref[rows:], moment_ref[...])
    twin = advanced(own_ref[rows:] + other_ref[:rows], twin_ref[...])[1]
    fresh_ref[...] = fresh
    blend_ref[...] = blend
    gram_ref[...] = packed_gram(gram_of(jnp.concatenate([blend, twin], axis=0)))


def plain_kernel(mine_ref, other_ref, moment_ref, fresh_ref, blend_ref, gram_ref):
    fresh, blend = advanced(mine_ref[...] + other_ref[...], moment_ref[...])
    fresh_ref[...] = fresh
    blend_ref[...] = blend
    gram_ref[...] = packed_gram(gram_of(blend))


def applied(value, factor):
    columns = factor.shape[1]
    left = jnp.concatenate(halves(value), axis=1)
    right = jnp.concatenate(halves(factor), axis=1)
    both = jnp.dot(left, jnp.concatenate([right, right], axis=0), preferred_element_type=jnp.float32)
    return both[:, columns:] + both[:, :columns]


def stacked(first, second):
    return tuple(jnp.concatenate(pair, axis=0) for pair in zip(first, second))


def newton_kernel(scale, n_grams, *refs):
    grams, blend_ref, update_ref, staged_ref, sems = refs[:n_grams], *refs[n_grams:]
    total = grams[0][...]
    for ref in grams[1:]:
        total = total + ref[...]
    gram = unpacked_gram(total)
    size = gram.shape[0]
    rows = lax.broadcasted_iota(jnp.int32, (size, size), 0)
    columns = lax.broadcasted_iota(jnp.int32, (size, size), 1)
    diagonal = rows == columns
    trace = jnp.sum(jnp.where(diagonal, gram, 0.0), axis=(0, 1), keepdims=True)
    inverse = 1.0 / (jnp.sqrt(trace) + epsilon)
    gram = gram * (inverse * inverse)
    start = jnp.where(diagonal, first_coef, 0.0)
    product = None
    for _ in range(ITERS - 1):
        split = thirds(gram)
        square = product_of(split, split)
        poly = start + second_coef * gram + third_coef * square
        factor = thirds(poly)
        if product is None:
            product, turned = poly, product_of(split, factor)
        else:
            both = product_of(stacked(split, thirds(product)), factor)
            turned, product = both[:size], both[size:]
        gram = product_of(thirds(turned), factor)
    split = thirds(gram)
    poly = start + second_coef * gram + third_coef * product_of(split, split)
    partway = applied(blend_ref[...], product * (inverse * scale))
    chunk = partway.shape[0] // 4
    copies = []
    for i in range(4):
        part = pl.ds(i * chunk, chunk)
        staged_ref[part, :] = applied(partway[i * chunk : (i + 1) * chunk], poly)
        copies.append(pltpu.make_async_copy(staged_ref.at[part], update_ref.at[part], sems.at[i]))
        copies[-1].start()
    for copy in copies:
        copy.wait()


def whole(count):
    return [pl.BlockSpec(memory_space=pltpu.VMEM) for _ in range(count)]


def on_chip(*arrays):
    return [pltpu.with_memory_space_constraint(array, pltpu.VMEM) for array in arrays]


def ordered(features, key_partials, momentum):
    n_fsdp = lax.axis_size("fsdp")
    n_tp = lax.axis_size("tp")
    parity = lax.axis_index("tp") % 2
    own_part = key_partials[:, 0, :]
    moment = momentum[:, 0, :]
    tokens, head_size = own_part.shape
    rows_half = moment.shape[0]
    bits = [1 << b for b in reversed(range(n_fsdp.bit_length() - 1))]
    direct = n_fsdp == 1 << len(bits) and n_fsdp <= 8 and rows_half % 128 == 0 and n_tp & (n_tp - 1) == 0
    block = pltpu.VMEM((rows_half, head_size), jnp.float32)
    small = pltpu.VMEM((head_size // 2 + 8, head_size), jnp.float32)
    if direct:
        n_chip = n_fsdp // 2
        gathered, stages = own_part, [own_part]
        packed = pltpu.VMEM((tokens, 2 * rows_half), features.dtype)
        for bit in bits[-2::-1]:
            stages.append(swapped(gathered, bit, 0))
            gathered = jnp.concatenate([gathered, stages[-1]], axis=0)
        pieces = pl.pallas_call(
            lambda *refs: pack_kernel(rows_half, *refs),
            out_shape=(packed,) * n_chip,
            in_specs=[pl.BlockSpec(memory_space=pl.ANY)],
            out_specs=tuple(whole(n_chip)),
            scratch_shapes=[pltpu.SemaphoreType.DMA((2 * n_chip,))],
            name="pack",
        )(features)
        pieces = list(pieces)
        for d in range(1, n_chip):
            pieces[d] = swapped(pieces[d], 2 * d, 0)
        partner_keys = swapped(gathered, 0, 1)
        twin = swapped(moment, 1, 0)
        partner_keys, twin = lax.optimization_barrier((partner_keys, twin))
        grads = pl.pallas_call(
            lambda *refs: partial_kernel(n_chip, *refs),
            out_shape=pltpu.VMEM((2 * rows_half, head_size), jnp.float32),
            in_specs=whole(n_chip + len(stages) + 1),
            out_specs=whole(1)[0],
            name="partial",
        )(*on_chip(*pieces, *stages, partner_keys))
        fresh, blend, gram = pl.pallas_call(
            joined_kernel,
            out_shape=(block, block, small),
            in_specs=whole(4),
            out_specs=tuple(whole(3)),
            name="gradient",
        )(*on_chip(grads, swapped(grads, 1, 0), moment, twin))
        others = []
        for d in reversed(range(1, n_chip)):
            others.append(swapped(gram, 2 * d, 0))
        for other in others:
            gram = gram + other
        grams = [gram, swapped(gram, 0, 1)]
    else:
        shard = lax.psum_scatter(
            lax.dot_general(features, own_part, contract, preferred_element_type=jnp.float32),
            "fsdp",
            scatter_dimension=0,
            tiled=True,
        )
        pair = shard.reshape(2, rows_half, head_size)
        mine = jnp.where(parity == 0, pair[0], pair[1])
        other = jnp.where(parity == 0, pair[1], pair[0])
        fresh, blend, gram = pl.pallas_call(
            plain_kernel,
            out_shape=(block, block, small),
            in_specs=whole(3),
            out_specs=tuple(whole(3)),
            name="gradient",
        )(*on_chip(mine, swapped(other, 0, 1), moment))
        gram = lax.psum(gram, "fsdp")
        grams = [gram, swapped(gram, 0, 1)]
    scale = shrink * math.sqrt(2 * n_fsdp * rows_half)
    update = pl.pallas_call(
        lambda *refs: newton_kernel(scale, len(grams), *refs),
        out_shape=jax.ShapeDtypeStruct((rows_half, head_size), jnp.float32),
        in_specs=whole(len(grams) + 1),
        out_specs=pl.BlockSpec(memory_space=pl.ANY),
        scratch_shapes=[pltpu.VMEM((rows_half, head_size), jnp.float32), pltpu.SemaphoreType.DMA((4,))],
        name="newton",
    )(*on_chip(*grams, blend))
    return (update[:, None, :], fresh[:, None, :])


def solution(mesh):
    placed = (P("fsdp", None), P("fsdp", "tp", None), P("fsdp", "tp", None))
    return jax.shard_map(
        ordered,
        mesh=mesh,
        in_specs=placed,
        out_specs=(P("fsdp", "tp", None), P("fsdp", "tp", None)),
        check_vma=False,
    )
```

```python
import math

import jax
import jax.numpy as jnp
from jax import lax
from jax.experimental import pallas as pl
from jax.experimental.pallas import tpu as pltpu
from jax.sharding import PartitionSpec as P


ITERS = 5


retain = 0.95
first_coef = 3.4445
second_coef = -4.775
third_coef = 2.0315
epsilon = 1e-07
shrink = 0.2
contract = (((0,), (0,)), ((), ()))


def swapped(block, fsdp_bits, tp_bits, odd_bits=None):
    n_tp = lax.axis_size("tp")
    count = lax.axis_size("fsdp") * n_tp
    choices = (fsdp_bits, fsdp_bits if odd_bits is None else odd_bits)
    masks = [choices[i // n_tp % 2] * n_tp + tp_bits for i in range(count)]
    return lax.ppermute(block, ("fsdp", "tp"), [(i, i ^ mask) for i, mask in enumerate(masks)])


def turned(distance, n_chip):
    width = n_chip.bit_length() - 1
    return sum((distance >> i & 1) << (width - 1 - i) for i in range(width))


def halves(value):
    high = value.astype(jnp.bfloat16)
    return high, (value - high.astype(jnp.float32)).astype(jnp.bfloat16)


def thirds(value):
    high = value.astype(jnp.bfloat16)
    rest = value - high.astype(jnp.float32)
    middle = rest.astype(jnp.bfloat16)
    return high, middle, (rest - middle.astype(jnp.float32)).astype(jnp.bfloat16)


def product_of(left, right):
    l1, l2, l3 = left
    r1, r2, r3 = right
    columns = r1.shape[1]
    square = jnp.concatenate([jnp.concatenate([r1, r2], 1), jnp.concatenate([r2, r1], 1)], 0)
    main = jnp.dot(jnp.concatenate([l1, l2], 1), square, preferred_element_type=jnp.float32)
    rest = jnp.dot(jnp.concatenate([l1, l3], 1), jnp.concatenate([r3, r1], 0), preferred_element_type=jnp.float32)
    return (rest + main[:, columns:]) + main[:, :columns]


def gram_of(value):
    width = value.shape[1]
    both = jnp.concatenate(halves(value), axis=1)
    parts = lax.dot_general(both, both, contract, preferred_element_type=jnp.float32)
    cross = parts[:width, width:] + parts[width:, :width]
    return (parts[width:, width:] + cross) + parts[:width, :width]


def packed_gram(gram):
    half = gram.shape[0] // 2
    upper, corner = gram[:half], gram[half:, half:]
    shape = (half, half)
    rows, columns = (lax.broadcasted_iota(jnp.int32, shape, axis) for axis in range(2))
    left = jnp.where(rows >= columns, upper[:, :half], corner)
    diagonal = jnp.sum(jnp.where(rows == columns, corner, 0.0), axis=0, keepdims=True)
    diagonal = jnp.broadcast_to(jnp.concatenate([diagonal, diagonal], axis=1), (8, 2 * half))
    return jnp.concatenate([jnp.concatenate([left, upper[:, half:]], axis=1), diagonal], axis=0)


def unpacked_gram(packed):
    half = packed.shape[1] // 2
    left, right, diagonal = packed[:half, :half], packed[:half, half:], packed[half : half + 1, :half]
    rows, columns = (lax.broadcasted_iota(jnp.int32, (half, half), axis) for axis in range(2))
    weight = jnp.where(rows == columns, 0.5, 1.0)
    first = jnp.where(rows >= columns, left * weight, 0.0)
    second = jnp.where(rows < columns, left, jnp.where(rows == columns, 0.5 * diagonal, 0.0))
    top = jnp.concatenate([first, right], axis=1)
    bottom = jnp.concatenate([jnp.zeros((half, half), jnp.float32), second], axis=1)
    triangle = jnp.concatenate([top, bottom], axis=0)
    return triangle + triangle.T


def advanced(grads, moment):
    fresh = retain * moment + grads
    return fresh, grads + retain * fresh


def far(distance):
    return distance & (distance - 1) != 0


def pack_kernel(width, features_ref, keys_ref, *refs):
    outs, sems = refs[:-1], refs[-1]
    index = lax.axis_index("fsdp")
    parity = lax.axis_index("tp") % 2
    chip, core = index // 2, index % 2
    copies = []
    for i, out in enumerate(outs):
        distance = jnp.where(core == 0, i, turned(i, len(outs)))
        for j in range(2):
            block = (chip ^ distance) * 2 + (core ^ j)
            start = pl.multiple_of((block * 2 + parity) * width, width)
            copies.append((features_ref.at[:, pl.ds(start, width)], out.at[:, pl.ds(j * width, width)]))
        if out.shape[1] > 2 * width:
            copies.append((keys_ref, out.at[:, pl.ds(2 * width, keys_ref.shape[1])]))
    copies = [pltpu.make_async_copy(*ends, sems.at[i]) for i, ends in enumerate(copies)]
    for copy in copies:
        copy.start()
    for copy in copies:
        copy.wait()


def partial_kernel(n_pieces, *refs):
    features, keys, grads_ref = refs[:n_pieces], list(refs[n_pieces:-1]), refs[-1]
    rows, head_size = grads_ref.shape
    own = [keys.pop(0)[...] if not i or far(i) else piece[:, rows:] for i, piece in enumerate(features)]
    partner = [ref[...] for ref in keys]
    keys = jnp.concatenate([jnp.concatenate(own, axis=0), jnp.concatenate(partner, axis=0)], axis=1)
    features = jnp.concatenate([piece[:, :rows] for piece in features], axis=0)
    both = lax.dot_general(features, keys, contract, preferred_element_type=jnp.float32)
    grads_ref[...] = both[:, :head_size] + both[:, head_size:]


def joined_kernel(own_ref, other_ref, moment_ref, twin_ref, fresh_ref, blend_ref, gram_ref):
    rows = moment_ref.shape[0]
    fresh, blend = advanced(own_ref[:rows] + other_ref[rows:], moment_ref[...])
    twin = advanced(own_ref[rows:] + other_ref[:rows], twin_ref[...])[1]
    fresh_ref[...] = fresh
    blend_ref[...] = blend
    gram_ref[...] = packed_gram(gram_of(jnp.concatenate([blend, twin], axis=0)))


def plain_kernel(mine_ref, other_ref, moment_ref, fresh_ref, blend_ref, gram_ref):
    fresh, blend = advanced(mine_ref[...] + other_ref[...], moment_ref[...])
    fresh_ref[...] = fresh
    blend_ref[...] = blend
    gram_ref[...] = packed_gram(gram_of(blend))


def applied(value, factor):
    columns = factor.shape[1]
    left = jnp.concatenate(halves(value), axis=1)
    right = jnp.concatenate(halves(factor), axis=1)
    both = jnp.dot(left, jnp.concatenate([right, right], axis=0), preferred_element_type=jnp.float32)
    return both[:, columns:] + both[:, :columns]


def stacked(first, second):
    return tuple(jnp.concatenate(pair, axis=0) for pair in zip(first, second))


def newton_kernel(scale, n_grams, *refs):
    grams, blend_ref, update_ref, staged_ref, sems = refs[:n_grams], *refs[n_grams:]
    total = grams[0][...]
    for ref in grams[1:]:
        total = total + ref[...]
    gram = unpacked_gram(total)
    size = gram.shape[0]
    rows = lax.broadcasted_iota(jnp.int32, (size, size), 0)
    columns = lax.broadcasted_iota(jnp.int32, (size, size), 1)
    diagonal = rows == columns
    trace = jnp.sum(jnp.where(diagonal, gram, 0.0), axis=(0, 1), keepdims=True)
    inverse = 1.0 / (jnp.sqrt(trace) + epsilon)
    scaling = inverse * inverse
    start = jnp.where(diagonal, first_coef, 0.0)
    split = thirds(gram)
    square = product_of(split, split)
    gram = gram * scaling
    split = thirds(gram)
    product = start + second_coef * gram + (third_coef * scaling) * (scaling * square)
    factor = thirds(product)
    gram = product_of(thirds(product_of(split, factor)), factor)
    for _ in range(ITERS - 2):
        split = thirds(gram)
        square = product_of(split, split)
        factor = thirds(start + second_coef * gram + third_coef * square)
        both = product_of(stacked(split, thirds(product)), factor)
        turned, product = both[:size], both[size:]
        gram = product_of(thirds(turned), factor)
    split = thirds(gram)
    poly = start + second_coef * gram + third_coef * product_of(split, split)
    partway = applied(blend_ref[...], product * (inverse * scale))
    chunk = partway.shape[0] // 4
    copies = []
    for i in range(4):
        part = pl.ds(i * chunk, chunk)
        staged_ref[part, :] = applied(partway[i * chunk : (i + 1) * chunk], poly)
        copies.append(pltpu.make_async_copy(staged_ref.at[part], update_ref.at[part], sems.at[i]))
        copies[-1].start()
    for copy in copies:
        copy.wait()


def whole(count):
    return [pl.BlockSpec(memory_space=pltpu.VMEM) for _ in range(count)]


def on_chip(*arrays):
    return [pltpu.with_memory_space_constraint(array, pltpu.VMEM) for array in arrays]


def ordered(features, key_partials, momentum):
    n_fsdp = lax.axis_size("fsdp")
    n_tp = lax.axis_size("tp")
    parity = lax.axis_index("tp") % 2
    own_part = key_partials[:, 0, :]
    moment = momentum[:, 0, :]
    tokens, head_size = own_part.shape
    rows_half = moment.shape[0]
    bits = [1 << b for b in reversed(range(n_fsdp.bit_length() - 1))]
    direct = n_fsdp == 1 << len(bits) and 4 <= n_fsdp <= 8 and rows_half % 128 == 0 and n_tp & (n_tp - 1) == 0
    block = pltpu.VMEM((rows_half, head_size), jnp.float32)
    small = pltpu.VMEM((head_size // 2 + 8, head_size), jnp.float32)
    if direct:
        n_chip = n_fsdp // 2
        wide = 2 * rows_half
        apart = [not d or far(d) for d in range(n_chip)]
        packed = [pltpu.VMEM((tokens, wide if alone else wide + head_size), features.dtype) for alone in apart]
        pieces = pl.pallas_call(
            lambda *refs: pack_kernel(rows_half, *refs),
            out_shape=tuple(packed),
            in_specs=[pl.BlockSpec(memory_space=pl.ANY)] * 2,
            out_specs=tuple(whole(n_chip)),
            scratch_shapes=[pltpu.SemaphoreType.DMA((3 * n_chip,))],
            name="pack",
        )(features, own_part)
        pieces, stages = list(pieces), [own_part]
        for d in range(1, n_chip):
            pieces[d] = swapped(pieces[d], 2 * d, 0, 2 * turned(d, n_chip))
            if apart[d]:
                stages.append(swapped(own_part, 2 * d, 0, 2 * turned(d, n_chip)))
        lone = list(stages)
        keys = [lone.pop(0) if apart[d] else pieces[d][:, wide:] for d in range(n_chip)]
        near_keys = jnp.concatenate([keys[d] for d in range(n_chip) if not far(d)], axis=0)
        partner_keys = [swapped(near_keys, 0, 1)]
        partner_keys += [swapped(keys[d], 0, 1) for d in range(n_chip) if far(d)]
        twin = swapped(moment, 1, 0)
        partner_keys[0], twin = lax.optimization_barrier((partner_keys[0], twin))
        grads = pl.pallas_call(
            lambda *refs: partial_kernel(n_chip, *refs),
            out_shape=pltpu.VMEM((2 * rows_half, head_size), jnp.float32),
            in_specs=whole(n_chip + len(stages) + len(partner_keys)),
            out_specs=whole(1)[0],
            name="partial",
        )(*on_chip(*pieces, *stages, *partner_keys))
        fresh, blend, gram = pl.pallas_call(
            joined_kernel,
            out_shape=(block, block, small),
            in_specs=whole(4),
            out_specs=tuple(whole(3)),
            name="gradient",
        )(*on_chip(grads, swapped(grads, 1, 0), moment, twin))
        others = []
        for d in reversed(range(1, n_chip)):
            others.append(swapped(gram, 2 * d, 0, 2 * turned(d, n_chip)))
        for other in others:
            gram = gram + other
        grams = [gram, swapped(gram, 0, 1)]
    else:
        shard = lax.psum_scatter(
            lax.dot_general(features, own_part, contract, preferred_element_type=jnp.float32),
            "fsdp",
            scatter_dimension=0,
            tiled=True,
        )
        pair = shard.reshape(2, rows_half, head_size)
        mine = jnp.where(parity == 0, pair[0], pair[1])
        other = jnp.where(parity == 0, pair[1], pair[0])
        fresh, blend, gram = pl.pallas_call(
            plain_kernel,
            out_shape=(block, block, small),
            in_specs=whole(3),
            out_specs=tuple(whole(3)),
            name="gradient",
        )(*on_chip(mine, swapped(other, 0, 1), moment))
        gram = lax.psum(gram, "fsdp")
        grams = [gram, swapped(gram, 0, 1)]
    scale = shrink * math.sqrt(2 * n_fsdp * rows_half)
    update = pl.pallas_call(
        lambda *refs: newton_kernel(scale, len(grams), *refs),
        out_shape=jax.ShapeDtypeStruct((rows_half, head_size), jnp.float32),
        in_specs=whole(len(grams) + 1),
        out_specs=pl.BlockSpec(memory_space=pl.ANY),
        scratch_shapes=[pltpu.VMEM((rows_half, head_size), jnp.float32), pltpu.SemaphoreType.DMA((4,))],
        name="newton",
    )(*on_chip(*grams, blend))
    return (update[:, None, :], fresh[:, None, :])


def solution(mesh):
    placed = (P("fsdp", None), P("fsdp", "tp", None), P("fsdp", "tp", None))
    return jax.shard_map(
        ordered,
        mesh=mesh,
        in_specs=placed,
        out_specs=(P("fsdp", "tp", None), P("fsdp", "tp", None)),
        check_vma=False,
    )
```

```python
import math

import jax
import jax.numpy as jnp
from jax import lax
from jax.experimental import pallas as pl
from jax.experimental.pallas import tpu as pltpu
from jax.sharding import PartitionSpec as P


ITERS = 5


retain = 0.95
first_coef = 3.4445
second_coef = -4.775
third_coef = 2.0315
epsilon = 1e-07
shrink = 0.2
contract = (((0,), (0,)), ((), ()))


def swapped(block, fsdp_bits, tp_bits, odd_bits=None):
    n_tp = lax.axis_size("tp")
    count = lax.axis_size("fsdp") * n_tp
    choices = (fsdp_bits, fsdp_bits if odd_bits is None else odd_bits)
    masks = [choices[i // n_tp % 2] * n_tp + tp_bits for i in range(count)]
    return lax.ppermute(block, ("fsdp", "tp"), [(i, i ^ mask) for i, mask in enumerate(masks)])


def turned(distance, n_chip):
    width = n_chip.bit_length() - 1
    return sum((distance >> i & 1) << (width - 1 - i) for i in range(width))


def halves(value):
    high = value.astype(jnp.bfloat16)
    return high, (value - high.astype(jnp.float32)).astype(jnp.bfloat16)


def thirds(value):
    high = value.astype(jnp.bfloat16)
    rest = value - high.astype(jnp.float32)
    middle = rest.astype(jnp.bfloat16)
    return high, middle, (rest - middle.astype(jnp.float32)).astype(jnp.bfloat16)


def product_of(left, right):
    l1, l2, l3 = left
    r1, r2, r3 = right
    columns = r1.shape[1]
    square = jnp.concatenate([jnp.concatenate([r1, r2], 1), jnp.concatenate([r2, r1], 1)], 0)
    main = jnp.dot(jnp.concatenate([l1, l2], 1), square, preferred_element_type=jnp.float32)
    rest = jnp.dot(jnp.concatenate([l1, l3], 1), jnp.concatenate([r3, r1], 0), preferred_element_type=jnp.float32)
    return (rest + main[:, columns:]) + main[:, :columns]


def gram_of(value):
    width = value.shape[1]
    both = jnp.concatenate(halves(value), axis=1)
    parts = lax.dot_general(both, both, contract, preferred_element_type=jnp.float32)
    cross = parts[:width, width:] + parts[width:, :width]
    return (parts[width:, width:] + cross) + parts[:width, :width]


def packed_gram(gram):
    half = gram.shape[0] // 2
    upper, corner = gram[:half], gram[half:, half:]
    shape = (half, half)
    rows, columns = (lax.broadcasted_iota(jnp.int32, shape, axis) for axis in range(2))
    left = jnp.where(rows >= columns, upper[:, :half], corner)
    diagonal = jnp.sum(jnp.where(rows == columns, corner, 0.0), axis=0, keepdims=True)
    diagonal = jnp.broadcast_to(jnp.concatenate([diagonal, diagonal], axis=1), (8, 2 * half))
    return jnp.concatenate([jnp.concatenate([left, upper[:, half:]], axis=1), diagonal], axis=0)


def unpacked_gram(packed):
    half = packed.shape[1] // 2
    left, right, diagonal = packed[:half, :half], packed[:half, half:], packed[half : half + 1, :half]
    rows, columns = (lax.broadcasted_iota(jnp.int32, (half, half), axis) for axis in range(2))
    weight = jnp.where(rows == columns, 0.5, 1.0)
    first = jnp.where(rows >= columns, left * weight, 0.0)
    second = jnp.where(rows < columns, left, jnp.where(rows == columns, 0.5 * diagonal, 0.0))
    top = jnp.concatenate([first, right], axis=1)
    bottom = jnp.concatenate([jnp.zeros((half, half), jnp.float32), second], axis=1)
    triangle = jnp.concatenate([top, bottom], axis=0)
    return triangle + triangle.T


def advanced(grads, moment):
    fresh = retain * moment + grads
    return fresh, grads + retain * fresh


def far(distance):
    return distance & (distance - 1) != 0


def pack_kernel(width, n_chip, slots, features_ref, keys_ref, *refs):
    outs, sems = refs[:-1], refs[-1]
    index = lax.axis_index("fsdp")
    parity = lax.axis_index("tp") % 2
    chip, core = index // 2, index % 2
    copies = []
    for i, out in zip(slots, outs):
        distance = jnp.where(core == 0, i, turned(i, n_chip))
        for j in range(2):
            block = (chip ^ distance) * 2 + (core ^ j)
            start = pl.multiple_of((block * 2 + parity) * width, width)
            copies.append((features_ref.at[:, pl.ds(start, width)], out.at[:, pl.ds(j * width, width)]))
        if out.shape[1] > 2 * width:
            copies.append((keys_ref, out.at[:, pl.ds(2 * width, keys_ref.shape[1])]))
    copies = [pltpu.make_async_copy(*ends, sems.at[i]) for i, ends in enumerate(copies)]
    for copy in copies:
        copy.start()
    for copy in copies:
        copy.wait()


def partial_kernel(n_pieces, *refs):
    features, keys, grads_ref = refs[:n_pieces], list(refs[n_pieces:-1]), refs[-1]
    rows, head_size = grads_ref.shape
    own = [keys.pop(0)[...] if not i or far(i) else piece[:, rows:] for i, piece in enumerate(features)]
    partner = [ref[...] for ref in keys]
    keys = jnp.concatenate([jnp.concatenate(own, axis=0), jnp.concatenate(partner, axis=0)], axis=1)
    features = jnp.concatenate([piece[:, :rows] for piece in features], axis=0)
    both = lax.dot_general(features, keys, contract, preferred_element_type=jnp.float32)
    grads_ref[...] = both[:, :head_size] + both[:, head_size:]


def joined_kernel(own_ref, other_ref, moment_ref, twin_ref, fresh_ref, blend_ref, gram_ref):
    rows = moment_ref.shape[0]
    fresh, blend = advanced(own_ref[:rows] + other_ref[rows:], moment_ref[...])
    twin = advanced(own_ref[rows:] + other_ref[:rows], twin_ref[...])[1]
    fresh_ref[...] = fresh
    blend_ref[...] = blend
    gram_ref[...] = packed_gram(gram_of(jnp.concatenate([blend, twin], axis=0)))


def plain_kernel(mine_ref, other_ref, moment_ref, fresh_ref, blend_ref, gram_ref):
    fresh, blend = advanced(mine_ref[...] + other_ref[...], moment_ref[...])
    fresh_ref[...] = fresh
    blend_ref[...] = blend
    gram_ref[...] = packed_gram(gram_of(blend))


def applied(value, factor):
    columns = factor.shape[1]
    left = jnp.concatenate(halves(value), axis=1)
    right = jnp.concatenate(halves(factor), axis=1)
    both = jnp.dot(left, jnp.concatenate([right, right], axis=0), preferred_element_type=jnp.float32)
    return both[:, columns:] + both[:, :columns]


def stacked(first, second):
    return tuple(jnp.concatenate(pair, axis=0) for pair in zip(first, second))


def newton_kernel(scale, n_grams, *refs):
    grams, blend_ref, update_ref, staged_ref, sems = refs[:n_grams], *refs[n_grams:]
    total = grams[0][...]
    for ref in grams[1:]:
        total = total + ref[...]
    gram = unpacked_gram(total)
    size = gram.shape[0]
    rows = lax.broadcasted_iota(jnp.int32, (size, size), 0)
    columns = lax.broadcasted_iota(jnp.int32, (size, size), 1)
    diagonal = rows == columns
    trace = jnp.sum(jnp.where(diagonal, gram, 0.0), axis=(0, 1), keepdims=True)
    inverse = 1.0 / (jnp.sqrt(trace) + epsilon)
    scaling = inverse * inverse
    start = jnp.where(diagonal, first_coef, 0.0)
    split = thirds(gram)
    square = product_of(split, split)
    gram = gram * scaling
    split = thirds(gram)
    product = start + second_coef * gram + (third_coef * scaling) * (scaling * square)
    factor = thirds(product)
    gram = product_of(thirds(product_of(split, factor)), factor)
    for _ in range(ITERS - 2):
        split = thirds(gram)
        square = product_of(split, split)
        factor = thirds(start + second_coef * gram + third_coef * square)
        both = product_of(stacked(split, thirds(product)), factor)
        turned, product = both[:size], both[size:]
        gram = product_of(thirds(turned), factor)
    split = thirds(gram)
    poly = start + second_coef * gram + third_coef * product_of(split, split)
    partway = applied(blend_ref[...], product * (inverse * scale))
    chunk = partway.shape[0] // 4
    copies = []
    for i in range(4):
        part = pl.ds(i * chunk, chunk)
        staged_ref[part, :] = applied(partway[i * chunk : (i + 1) * chunk], poly)
        copies.append(pltpu.make_async_copy(staged_ref.at[part], update_ref.at[part], sems.at[i]))
        copies[-1].start()
    for copy in copies:
        copy.wait()


def whole(count):
    return [pl.BlockSpec(memory_space=pltpu.VMEM) for _ in range(count)]


def on_chip(*arrays):
    return [pltpu.with_memory_space_constraint(array, pltpu.VMEM) for array in arrays]


def ordered(features, key_partials, momentum):
    n_fsdp = lax.axis_size("fsdp")
    n_tp = lax.axis_size("tp")
    parity = lax.axis_index("tp") % 2
    own_part = key_partials[:, 0, :]
    moment = momentum[:, 0, :]
    tokens, head_size = own_part.shape
    rows_half = moment.shape[0]
    bits = [1 << b for b in reversed(range(n_fsdp.bit_length() - 1))]
    direct = n_fsdp == 1 << len(bits) and 4 <= n_fsdp <= 8 and rows_half % 128 == 0 and n_tp & (n_tp - 1) == 0
    block = pltpu.VMEM((rows_half, head_size), jnp.float32)
    small = pltpu.VMEM((head_size // 2 + 8, head_size), jnp.float32)
    if direct:
        n_chip = n_fsdp // 2
        wide = 2 * rows_half
        apart = [not d or far(d) for d in range(n_chip)]
        packed = [pltpu.VMEM((tokens, wide if alone else wide + head_size), features.dtype) for alone in apart]
        pieces = [None] * n_chip
        for slots in ([1], [2], list(range(3, n_chip)), [0]):
            if not slots:
                continue
            arrays = pl.pallas_call(
                lambda *refs, slots=slots: pack_kernel(rows_half, n_chip, slots, *refs),
                out_shape=tuple(packed[d] for d in slots),
                in_specs=[pl.BlockSpec(memory_space=pl.ANY)] * 2,
                out_specs=tuple(whole(len(slots))),
                scratch_shapes=[pltpu.SemaphoreType.DMA((3 * len(slots),))],
            )(features, own_part)
            for d, array in zip(slots, arrays):
                pieces[d] = array
        stages = [own_part]
        for d in range(1, n_chip):
            pieces[d] = swapped(pieces[d], 2 * d, 0, 2 * turned(d, n_chip))
            if apart[d]:
                stages.append(swapped(own_part, 2 * d, 0, 2 * turned(d, n_chip)))
        lone = list(stages)
        keys = [lone.pop(0) if apart[d] else pieces[d][:, wide:] for d in range(n_chip)]
        near_keys = jnp.concatenate([keys[d] for d in range(n_chip) if not far(d)], axis=0)
        partner_keys = [swapped(near_keys, 0, 1)]
        partner_keys += [swapped(keys[d], 0, 1) for d in range(n_chip) if far(d)]
        twin = swapped(moment, 1, 0)
        partner_keys[0], twin = lax.optimization_barrier((partner_keys[0], twin))
        grads = pl.pallas_call(
            lambda *refs: partial_kernel(n_chip, *refs),
            out_shape=pltpu.VMEM((2 * rows_half, head_size), jnp.float32),
            in_specs=whole(n_chip + len(stages) + len(partner_keys)),
            out_specs=whole(1)[0],
            name="partial",
        )(*on_chip(*pieces, *stages, *partner_keys))
        fresh, blend, gram = pl.pallas_call(
            joined_kernel,
            out_shape=(block, block, small),
            in_specs=whole(4),
            out_specs=tuple(whole(3)),
            name="gradient",
        )(*on_chip(grads, swapped(grads, 1, 0), moment, twin))
        others = []
        for d in reversed(range(1, n_chip)):
            others.append(swapped(gram, 2 * d, 0, 2 * turned(d, n_chip)))
        for other in others:
            gram = gram + other
        grams = [gram, swapped(gram, 0, 1)]
    else:
        shard = lax.psum_scatter(
            lax.dot_general(features, own_part, contract, preferred_element_type=jnp.float32),
            "fsdp",
            scatter_dimension=0,
            tiled=True,
        )
        pair = shard.reshape(2, rows_half, head_size)
        mine = jnp.where(parity == 0, pair[0], pair[1])
        other = jnp.where(parity == 0, pair[1], pair[0])
        fresh, blend, gram = pl.pallas_call(
            plain_kernel,
            out_shape=(block, block, small),
            in_specs=whole(3),
            out_specs=tuple(whole(3)),
            name="gradient",
        )(*on_chip(mine, swapped(other, 0, 1), moment))
        gram = lax.psum(gram, "fsdp")
        grams = [gram, swapped(gram, 0, 1)]
    scale = shrink * math.sqrt(2 * n_fsdp * rows_half)
    update = pl.pallas_call(
        lambda *refs: newton_kernel(scale, len(grams), *refs),
        out_shape=jax.ShapeDtypeStruct((rows_half, head_size), jnp.float32),
        in_specs=whole(len(grams) + 1),
        out_specs=pl.BlockSpec(memory_space=pl.ANY),
        scratch_shapes=[pltpu.VMEM((rows_half, head_size), jnp.float32), pltpu.SemaphoreType.DMA((4,))],
        name="newton",
    )(*on_chip(*grams, blend))
    return (update[:, None, :], fresh[:, None, :])


def solution(mesh):
    placed = (P("fsdp", None), P("fsdp", "tp", None), P("fsdp", "tp", None))
    return jax.shard_map(
        ordered,
        mesh=mesh,
        in_specs=placed,
        out_specs=(P("fsdp", "tp", None), P("fsdp", "tp", None)),
        check_vma=False,
    )
```

```python
import math

import jax
import jax.numpy as jnp
from jax import lax
from jax.experimental import pallas as pl
from jax.experimental.pallas import tpu as pltpu
from jax.sharding import PartitionSpec as P


ITERS = 5


retain = 0.95
first_coef = 3.4445
second_coef = -4.775
third_coef = 2.0315
epsilon = 1e-07
shrink = 0.2
contract = (((0,), (0,)), ((), ()))


def swapped(block, fsdp_bits, tp_bits, odd_bits=None):
    n_tp = lax.axis_size("tp")
    count = lax.axis_size("fsdp") * n_tp
    choices = (fsdp_bits, fsdp_bits if odd_bits is None else odd_bits)
    masks = [choices[i // n_tp % 2] * n_tp + tp_bits for i in range(count)]
    return lax.ppermute(block, ("fsdp", "tp"), [(i, i ^ mask) for i, mask in enumerate(masks)])


def turned(distance, n_chip):
    width = n_chip.bit_length() - 1
    return sum((distance >> i & 1) << (width - 1 - i) for i in range(width))


def halves(value):
    high = value.astype(jnp.bfloat16)
    return high, (value - high.astype(jnp.float32)).astype(jnp.bfloat16)


def thirds(value):
    high = value.astype(jnp.bfloat16)
    rest = value - high.astype(jnp.float32)
    middle = rest.astype(jnp.bfloat16)
    return high, middle, (rest - middle.astype(jnp.float32)).astype(jnp.bfloat16)


def product_of(left, right):
    l1, l2, l3 = left
    r1, r2, r3 = right
    columns = r1.shape[1]
    square = jnp.concatenate([jnp.concatenate([r1, r2], 1), jnp.concatenate([r2, r1], 1)], 0)
    main = jnp.dot(jnp.concatenate([l1, l2], 1), square, preferred_element_type=jnp.float32)
    rest = jnp.dot(jnp.concatenate([l1, l3], 1), jnp.concatenate([r3, r1], 0), preferred_element_type=jnp.float32)
    return (rest + main[:, columns:]) + main[:, :columns]


def gram_of(value):
    width = value.shape[1]
    both = jnp.concatenate(halves(value), axis=1)
    parts = lax.dot_general(both, both, contract, preferred_element_type=jnp.float32)
    cross = parts[:width, width:] + parts[width:, :width]
    return (parts[width:, width:] + cross) + parts[:width, :width]


def packed_gram(gram):
    half = gram.shape[0] // 2
    upper, corner = gram[:half], gram[half:, half:]
    shape = (half, half)
    rows, columns = (lax.broadcasted_iota(jnp.int32, shape, axis) for axis in range(2))
    left = jnp.where(rows >= columns, upper[:, :half], corner)
    diagonal = jnp.sum(jnp.where(rows == columns, corner, 0.0), axis=0, keepdims=True)
    diagonal = jnp.broadcast_to(jnp.concatenate([diagonal, diagonal], axis=1), (8, 2 * half))
    return jnp.concatenate([jnp.concatenate([left, upper[:, half:]], axis=1), diagonal], axis=0)


def unpacked_gram(packed):
    half = packed.shape[1] // 2
    left, right, diagonal = packed[:half, :half], packed[:half, half:], packed[half : half + 1, :half]
    rows, columns = (lax.broadcasted_iota(jnp.int32, (half, half), axis) for axis in range(2))
    weight = jnp.where(rows == columns, 0.5, 1.0)
    first = jnp.where(rows >= columns, left * weight, 0.0)
    second = jnp.where(rows < columns, left, jnp.where(rows == columns, 0.5 * diagonal, 0.0))
    top = jnp.concatenate([first, right], axis=1)
    bottom = jnp.concatenate([jnp.zeros((half, half), jnp.float32), second], axis=1)
    triangle = jnp.concatenate([top, bottom], axis=0)
    return triangle + triangle.T


def advanced(grads, moment):
    fresh = retain * moment + grads
    return fresh, grads + retain * fresh


def far(distance):
    return distance & (distance - 1) != 0


def pack_kernel(width, n_chip, slots, features_ref, keys_ref, *refs):
    outs, sems = refs[:-1], refs[-1]
    index = lax.axis_index("fsdp")
    parity = lax.axis_index("tp") % 2
    chip, core = index // 2, index % 2
    copies = []
    for i, out in zip(slots, outs):
        distance = jnp.where(core == 0, i, turned(i, n_chip))
        for j in range(2):
            block = (chip ^ distance) * 2 + (core ^ j)
            start = pl.multiple_of((block * 2 + parity) * width, width)
            copies.append((features_ref.at[:, pl.ds(start, width)], out.at[:, pl.ds(j * width, width)]))
        if out.shape[1] > 2 * width:
            copies.append((keys_ref, out.at[:, pl.ds(2 * width, keys_ref.shape[1])]))
    copies = [pltpu.make_async_copy(*ends, sems.at[i]) for i, ends in enumerate(copies)]
    for copy in copies:
        copy.start()
    for copy in copies:
        copy.wait()


def product_sum(pieces, own, partner, head_size):
    keys = jnp.concatenate([jnp.concatenate(own, axis=0), partner], axis=1)
    both = lax.dot_general(jnp.concatenate(pieces, axis=0), keys, contract, preferred_element_type=jnp.float32)
    return both[:, :head_size] + both[:, head_size:]


def near_kernel(*refs):
    pieces, own_ref, partner_ref, grads_ref = refs[:-3], *refs[-3:]
    rows, head_size = grads_ref.shape
    own = [own_ref[...]] + [piece[:, rows:] for piece in pieces[1:]]
    grads_ref[...] = product_sum([piece[:, :rows] for piece in pieces], own, partner_ref[...], head_size)


def far_kernel(near_ref, piece_ref, own_ref, partner_ref, grads_ref):
    head_size = grads_ref.shape[1]
    grads_ref[...] = near_ref[...] + product_sum([piece_ref[...]], [own_ref[...]], partner_ref[...], head_size)


def joined_kernel(own_ref, other_ref, moment_ref, twin_ref, fresh_ref, blend_ref, gram_ref):
    rows = moment_ref.shape[0]
    fresh, blend = advanced(own_ref[:rows] + other_ref[rows:], moment_ref[...])
    twin = advanced(own_ref[rows:] + other_ref[:rows], twin_ref[...])[1]
    fresh_ref[...] = fresh
    blend_ref[...] = blend
    gram_ref[...] = packed_gram(gram_of(jnp.concatenate([blend, twin], axis=0)))


def plain_kernel(mine_ref, other_ref, moment_ref, fresh_ref, blend_ref, gram_ref):
    fresh, blend = advanced(mine_ref[...] + other_ref[...], moment_ref[...])
    fresh_ref[...] = fresh
    blend_ref[...] = blend
    gram_ref[...] = packed_gram(gram_of(blend))


def applied(value, factor):
    columns = factor.shape[1]
    left = jnp.concatenate(halves(value), axis=1)
    right = jnp.concatenate(halves(factor), axis=1)
    both = jnp.dot(left, jnp.concatenate([right, right], axis=0), preferred_element_type=jnp.float32)
    return both[:, columns:] + both[:, :columns]


def stacked(first, second):
    return tuple(jnp.concatenate(pair, axis=0) for pair in zip(first, second))


def newton_kernel(scale, n_grams, *refs):
    grams, blend_ref, update_ref, staged_ref, sems = refs[:n_grams], *refs[n_grams:]
    total = grams[0][...]
    for ref in grams[1:]:
        total = total + ref[...]
    gram = unpacked_gram(total)
    size = gram.shape[0]
    rows = lax.broadcasted_iota(jnp.int32, (size, size), 0)
    columns = lax.broadcasted_iota(jnp.int32, (size, size), 1)
    diagonal = rows == columns
    trace = jnp.sum(jnp.where(diagonal, gram, 0.0), axis=(0, 1), keepdims=True)
    inverse = 1.0 / (jnp.sqrt(trace) + epsilon)
    scaling = inverse * inverse
    start = jnp.where(diagonal, first_coef, 0.0)
    split = thirds(gram)
    square = product_of(split, split)
    gram = gram * scaling
    split = thirds(gram)
    product = start + second_coef * gram + (third_coef * scaling) * (scaling * square)
    factor = thirds(product)
    gram = product_of(thirds(product_of(split, factor)), factor)
    for _ in range(ITERS - 2):
        split = thirds(gram)
        square = product_of(split, split)
        factor = thirds(start + second_coef * gram + third_coef * square)
        both = product_of(stacked(split, thirds(product)), factor)
        turned, product = both[:size], both[size:]
        gram = product_of(thirds(turned), factor)
    split = thirds(gram)
    poly = start + second_coef * gram + third_coef * product_of(split, split)
    partway = applied(blend_ref[...], product * (inverse * scale))
    chunk = partway.shape[0] // 4
    copies = []
    for i in range(4):
        part = pl.ds(i * chunk, chunk)
        staged_ref[part, :] = applied(partway[i * chunk : (i + 1) * chunk], poly)
        copies.append(pltpu.make_async_copy(staged_ref.at[part], update_ref.at[part], sems.at[i]))
        copies[-1].start()
    for copy in copies:
        copy.wait()


def whole(count):
    return [pl.BlockSpec(memory_space=pltpu.VMEM) for _ in range(count)]


def on_chip(*arrays):
    return [pltpu.with_memory_space_constraint(array, pltpu.VMEM) for array in arrays]


def ordered(features, key_partials, momentum):
    n_fsdp = lax.axis_size("fsdp")
    n_tp = lax.axis_size("tp")
    parity = lax.axis_index("tp") % 2
    own_part = key_partials[:, 0, :]
    moment = momentum[:, 0, :]
    tokens, head_size = own_part.shape
    rows_half = moment.shape[0]
    bits = [1 << b for b in reversed(range(n_fsdp.bit_length() - 1))]
    direct = n_fsdp == 1 << len(bits) and 4 <= n_fsdp <= 8 and rows_half % 128 == 0 and n_tp & (n_tp - 1) == 0
    block = pltpu.VMEM((rows_half, head_size), jnp.float32)
    small = pltpu.VMEM((head_size // 2 + 8, head_size), jnp.float32)
    if direct:
        n_chip = n_fsdp // 2
        wide = 2 * rows_half
        apart = [not d or far(d) for d in range(n_chip)]
        packed = [pltpu.VMEM((tokens, wide if alone else wide + head_size), features.dtype) for alone in apart]
        pieces = [None] * n_chip
        for slots in ([1], [2], list(range(3, n_chip)), [0]):
            if not slots:
                continue
            arrays = pl.pallas_call(
                lambda *refs, slots=slots: pack_kernel(rows_half, n_chip, slots, *refs),
                out_shape=tuple(packed[d] for d in slots),
                in_specs=[pl.BlockSpec(memory_space=pl.ANY)] * 2,
                out_specs=tuple(whole(len(slots))),
                scratch_shapes=[pltpu.SemaphoreType.DMA((3 * len(slots),))],
            )(features, own_part)
            for d, array in zip(slots, arrays):
                pieces[d] = array
        stages = [own_part]
        for d in range(1, n_chip):
            pieces[d] = swapped(pieces[d], 2 * d, 0, 2 * turned(d, n_chip))
            if apart[d]:
                stages.append(swapped(own_part, 2 * d, 0, 2 * turned(d, n_chip)))
        lone = list(stages)
        keys = [lone.pop(0) if apart[d] else pieces[d][:, wide:] for d in range(n_chip)]
        near_keys = jnp.concatenate([keys[d] for d in range(n_chip) if not far(d)], axis=0)
        partner_keys = [swapped(near_keys, 0, 1)]
        partner_keys += [swapped(keys[d], 0, 1) for d in range(n_chip) if far(d)]
        twin = swapped(moment, 1, 0)
        partner_keys[0], twin = lax.optimization_barrier((partner_keys[0], twin))
        total = pltpu.VMEM((2 * rows_half, head_size), jnp.float32)
        near = [pieces[d] for d in range(n_chip) if not far(d)]
        grads = pl.pallas_call(
            near_kernel,
            out_shape=total,
            in_specs=whole(len(near) + 2),
            out_specs=whole(1)[0],
            name="near",
        )(*on_chip(*near, own_part, partner_keys[0]))
        distant = [pieces[d] for d in range(n_chip) if far(d)]
        for piece, own, partner in zip(distant, stages[1:], partner_keys[1:]):
            grads = pl.pallas_call(
                far_kernel,
                out_shape=total,
                in_specs=whole(4),
                out_specs=whole(1)[0],
                name="far",
            )(*on_chip(grads, piece, own, partner))
        fresh, blend, gram = pl.pallas_call(
            joined_kernel,
            out_shape=(block, block, small),
            in_specs=whole(4),
            out_specs=tuple(whole(3)),
            name="gradient",
        )(*on_chip(grads, swapped(grads, 1, 0), moment, twin))
        others = []
        for d in reversed(range(1, n_chip)):
            others.append(swapped(gram, 2 * d, 0, 2 * turned(d, n_chip)))
        for other in others:
            gram = gram + other
        grams = [gram, swapped(gram, 0, 1)]
    else:
        shard = lax.psum_scatter(
            lax.dot_general(features, own_part, contract, preferred_element_type=jnp.float32),
            "fsdp",
            scatter_dimension=0,
            tiled=True,
        )
        pair = shard.reshape(2, rows_half, head_size)
        mine = jnp.where(parity == 0, pair[0], pair[1])
        other = jnp.where(parity == 0, pair[1], pair[0])
        fresh, blend, gram = pl.pallas_call(
            plain_kernel,
            out_shape=(block, block, small),
            in_specs=whole(3),
            out_specs=tuple(whole(3)),
            name="gradient",
        )(*on_chip(mine, swapped(other, 0, 1), moment))
        gram = lax.psum(gram, "fsdp")
        grams = [gram, swapped(gram, 0, 1)]
    scale = shrink * math.sqrt(2 * n_fsdp * rows_half)
    update = pl.pallas_call(
        lambda *refs: newton_kernel(scale, len(grams), *refs),
        out_shape=jax.ShapeDtypeStruct((rows_half, head_size), jnp.float32),
        in_specs=whole(len(grams) + 1),
        out_specs=pl.BlockSpec(memory_space=pl.ANY),
        scratch_shapes=[pltpu.VMEM((rows_half, head_size), jnp.float32), pltpu.SemaphoreType.DMA((4,))],
        name="newton",
    )(*on_chip(*grams, blend))
    return (update[:, None, :], fresh[:, None, :])


def solution(mesh):
    placed = (P("fsdp", None), P("fsdp", "tp", None), P("fsdp", "tp", None))
    return jax.shard_map(
        ordered,
        mesh=mesh,
        in_specs=placed,
        out_specs=(P("fsdp", "tp", None), P("fsdp", "tp", None)),
        check_vma=False,
    )
```
